128 devices in a mesh: ctx: 16 (over y_hi, x, core), vocab: 8 (over y_lo, z).
Axes of the slice: x: 4, y: 4 (y_hi: 2, y_lo: 2; y = y_hi * 2 + y_lo), z: 4, core: 2. Of those that a mesh axis runs over, the one named last changes fastest.
Arguments:
- block_query: bfloat16 [512, 6144], P('ctx', 'vocab'), may hold values from -16 to 16
- block_key: bfloat16 [512, 6144], P('ctx', 'vocab'), may hold values from -16 to 16
- block_value: bfloat16 [512, 6144], P('ctx', 'vocab'), may hold values from -6 to 6
- block_doc: int32 [512], P('ctx'), may hold values from 0 to 1, never falling along the last dimension, each value on 1 to 480 neighbouring positions
- token_query: bfloat16 [2048, 6144], P(('ctx', 'vocab')), may hold values from -16 to 16
- token_key: bfloat16 [2048, 6144], P(('ctx', 'vocab')), may hold values from -16 to 16
- token_value: bfloat16 [2048, 6144], P(('ctx', 'vocab')), may hold values from -600 to 600
- token_state: bfloat16 [2048, 6144], P(('ctx', 'vocab')), may hold values from -6 to 6
- norm_gain: float32 [6144], replicated, may hold values from 0.5 to 1.5
- head_weight: bfloat16 [6144, 131072], P(None, ('ctx', 'vocab')), may hold values from -128 to 128
- targets: int32 [2048], replicated, may hold values from 0 to 131071
Outputs:
- block_context: bfloat16 [512, 6144], P('ctx', 'vocab')
- token_prior: float32 [2048], P(('ctx', 'vocab'))
The draws below stay inside these ranges and needn't reach their ends.
Inputs may be any that keep to these rules, and one draw needn't show every extreme that they name: block_doc never falls along the blocks; no document holds more than 480 blocks.
All inputs are finite; a program needn't handle non-finite values.
Results may differ from the reference program's by a relative error of at most 0.005.
Values may be sent and summed in bfloat16 or wider, within the bound.
No kernel may reach another device: no remote copies, remote signals or barrier semaphores. Data moves between devices by JAX's collectives and lax.ppermute only.
A program may use at most 128 MiB of HBM per device.

```python
import math
import jax
import jax.numpy as jnp
import numpy as np
from jax import lax

HEADS = 48
HEAD_DIM = 128
BLOCK_LEN = 4
DOCS = 2
BLK_DEV = 32
WIDTH = 6144
BLOCKS = 512
TOKENS = 2048
VOCAB = 131072


def noise(key, salt, rows):
    return jnp.clip(jax.random.normal(jax.random.fold_in(key, salt), (rows, WIDTH), jnp.float32), -6.0, 6.0)


def draw_block_query(key, part):
    base = noise(key, 11, BLOCKS)
    return base.astype(jnp.bfloat16)


def draw_block_key(key, part):
    base = noise(key, 12, BLOCKS)
    return base.astype(jnp.bfloat16)


def draw_token_query(key, part):
    base = noise(key, 21, TOKENS)
    return base.astype(jnp.bfloat16)


def draw_token_key(key, part):
    base = noise(key, 22, TOKENS)
    return base.astype(jnp.bfloat16)


def draw_token_value(key, part):
    base = noise(key, 23, TOKENS)
    return base.astype(jnp.bfloat16)


def draw_head_weight(key, part):
    column = jnp.arange(VOCAB, dtype=jnp.float32)
    spread = 3.0 / math.sqrt(WIDTH) * (0.6 + 1.2 * column / VOCAB)
    base = jnp.clip(jax.random.normal(jax.random.fold_in(key, 31), (WIDTH, VOCAB), jnp.float32), -6.0, 6.0) * spread[None, :]
    return base.astype(jnp.bfloat16)


def place_ends(values, rng, least, top_value):
    extent = values.shape
    spot = [jax.random.randint(jax.random.fold_in(rng, axis), (), 0, extent[axis]) for axis in range(len(extent))]
    values = values.at[tuple(spot)].set(least)
    longest = extent.index(max(extent))
    spot[longest] = (spot[longest] + 1) % extent[longest]
    return values.at[tuple(spot)].set(top_value)


def shard_levels(rng, shape, pieces, least, top_value):
    gain, own = 1.0, jax.random.fold_in(rng, 6)
    for axis_at, shards_of in pieces:
        heights = jnp.exp(jax.random.uniform(jax.random.fold_in(own, axis_at), (shards_of,), jnp.float32, least / len(pieces), top_value / len(pieces)))
        gain = gain * jnp.repeat(heights, shape[axis_at] // shards_of).reshape([-1 if axis == axis_at else 1 for axis in range(len(shape))])
    return gain


def skewed_wide(rng, dims, count, slope):
    weights = [min(1 << octave, count + 1 - (1 << octave)) * (1 << 20) // math.isqrt((1 << octave) ** slope) + 1 for octave in range((count + 1).bit_length()) if 1 << octave <= count]
    scale = 1 + sum(weights) // (1 << 30)
    grid = np.cumsum(np.array([max(1, weight // scale) for weight in weights]))
    lot = jax.random.randint(jax.random.fold_in(rng, 1), dims, 0, int(grid[len(weights) - 1]))
    start = jnp.left_shift(1, jnp.searchsorted(jnp.asarray(grid, jnp.int32), lot, side="right").astype(jnp.int32))
    standing = start - 1 + jax.random.randint(jax.random.fold_in(rng, 4), dims, 0, 1 << 30) % jnp.minimum(start, count + 1 - start)
    return jax.random.permutation(jax.random.fold_in(rng, 2), count)[standing].astype(jnp.int32)


def profile(number_of, total, bound, slope):
    weights = [(1 << 20) // math.isqrt(rank ** slope) + 1 for rank in range(2, number_of + 1)]
    surplus, given = total - bound - (number_of - 1), [1] * (number_of - 1)
    while surplus > 0:
        free = [i for i in range(number_of - 1) if given[i] < bound]
        mass, left = sum([weights[i] for i in free]), surplus
        for i in free:
            extra = min(bound - given[i], max(1, left * weights[i] // mass), surplus)
            given[i] = given[i] + extra
            surplus = surplus - extra
    return np.array([bound] + given)


def ragged_sizes(own_key, amount, total, bound, skew):
    if amount == 2:
        one = jax.random.randint(own_key, (), max(1, total - bound), min(bound, total - 1) + 1)
        return jnp.stack([one, total - one])
    lengths = jnp.asarray(profile(amount, total, bound, skew), jnp.int32)
    twos = (amount - 1) // 2
    donor, taker = lengths[1:1 + 2 * twos:2], lengths[2:2 + 2 * twos:2]
    room = jnp.minimum(donor - 1, bound - taker)
    passed = jax.random.randint(jax.random.fold_in(own_key, 1), (twos,), 0, 1 << 20) % (room + 1)
    lengths = lengths.at[1:1 + 2 * twos:2].set(donor - passed).at[2:2 + 2 * twos:2].set(taker + passed)
    return lengths[jax.random.permutation(jax.random.fold_in(own_key, 2), amount)]


def normal_values(stream_key, extent, width, bound, pieces=(), kind=jnp.bfloat16):
    array = jax.random.normal(stream_key, extent, jnp.float32) * width
    if len(pieces) > 0:
        array = shard_levels(stream_key, extent, pieces, -0.22, 0.18) * array
    return jnp.clip(array, min=-bound, max=bound).astype(kind)


def setup_inputs(seed: int = 0) -> dict:
    arg_keys = jax.random.split(jax.random.key(seed), 12)
    block_query = draw_block_query(jax.random.fold_in(arg_keys[11], 71), 0)
    block_key = draw_block_key(jax.random.fold_in(arg_keys[11], 71), 0)
    block_value = normal_values(arg_keys[2], (BLOCKS, WIDTH), 1.0, 6.0, ((0, 16), (1, 8)))
    block_doc = jnp.searchsorted(jnp.cumsum(ragged_sizes(arg_keys[3], DOCS, BLOCKS, BLOCKS - BLK_DEV, 0)), jnp.arange(BLOCKS), side="right").astype(jnp.int32)
    token_query = draw_token_query(jax.random.fold_in(arg_keys[11], 71), 0)
    token_key = draw_token_key(jax.random.fold_in(arg_keys[11], 71), 0)
    token_value = draw_token_value(jax.random.fold_in(arg_keys[11], 71), 0)
    token_state = normal_values(arg_keys[7], (TOKENS, WIDTH), 1.0, 6.0, ((0, 128),))
    norm_gain = jnp.clip(1.0 + 0.1 * jax.random.normal(arg_keys[8], (WIDTH,), jnp.float32), 0.5, 1.5)
    head_weight = draw_head_weight(jax.random.fold_in(arg_keys[11], 71), 0)
    targets = place_ends(skewed_wide(arg_keys[10], (TOKENS,), VOCAB, 2), jax.random.fold_in(arg_keys[10], 3), 0, VOCAB - 1).astype(jnp.int32)
    return dict(block_query=block_query, block_key=block_key, block_value=block_value, block_doc=block_doc, token_query=token_query, token_key=token_key, token_value=token_value, token_state=token_state, norm_gain=norm_gain, head_weight=head_weight, targets=targets)


def global_mixing(block_query, block_key, block_value, block_doc):
    scale = 1.0 / math.sqrt(HEAD_DIM)
    queries = block_query.reshape(BLOCKS, HEADS, HEAD_DIM).astype(jnp.float32)
    keys = block_key.reshape(BLOCKS, HEADS, HEAD_DIM).astype(jnp.float32)
    values = block_value.reshape(BLOCKS, HEADS, HEAD_DIM).astype(jnp.float32)
    scores = jnp.einsum('qhd,khd->qhk', queries, keys) * scale
    places = jnp.arange(BLOCKS, dtype=jnp.int32)
    allowed = (places[:, None] >= places[None, :]) & (block_doc[:, None] == block_doc[None, :])
    scores = jnp.where(allowed[:, None, :], scores, -jnp.inf)
    highest = lax.optimization_barrier(jnp.max(scores, axis=-1, keepdims=True))
    weights = jnp.exp(scores - highest)
    totals = lax.optimization_barrier(jnp.sum(weights, axis=-1))
    rounded = lax.optimization_barrier(weights.astype(jnp.bfloat16)).astype(jnp.float32)
    mixed = jnp.einsum('qhk,khd->qhd', rounded, values) / totals[:, :, None]
    return mixed.reshape(BLOCKS, WIDTH).astype(jnp.bfloat16)

def local_decoder(context, token_query, token_key, token_value, token_state, norm_gain):
    scale = 1.0 / math.sqrt(HEAD_DIM)
    groups = context.shape[0]
    shape = (groups, BLOCK_LEN, HEADS, HEAD_DIM)
    prefix = context.reshape(groups, 1, HEADS, HEAD_DIM)
    queries = token_query.reshape(shape).astype(jnp.float32)
    keys = jnp.concatenate([prefix, token_key.reshape(shape)], axis=1).astype(jnp.float32)
    values = jnp.concatenate([prefix, token_value.reshape(shape)], axis=1).astype(jnp.float32)
    scores = jnp.einsum('bihd,bjhd->bhij', queries, keys) * scale
    allowed = jnp.arange(BLOCK_LEN + 1, dtype=jnp.int32)[None, :] <= jnp.arange(BLOCK_LEN, dtype=jnp.int32)[:, None] + 1
    scores = jnp.where(allowed, scores, -jnp.inf)
    highest = lax.optimization_barrier(jnp.max(scores, axis=-1, keepdims=True))
    weights = jnp.exp(scores - highest)
    totals = lax.optimization_barrier(jnp.sum(weights, axis=-1))
    rounded = lax.optimization_barrier(weights.astype(jnp.bfloat16)).astype(jnp.float32)
    mixed = jnp.einsum('bhij,bjhd->bihd', rounded, values) / jnp.transpose(totals, (0, 2, 1))[..., None]
    summed = token_state.astype(jnp.float32) + mixed.reshape(groups * BLOCK_LEN, WIDTH)
    power = lax.optimization_barrier(jnp.mean(summed * summed, axis=-1, keepdims=True))
    return (summed * lax.rsqrt(power + 1e-05) * norm_gain).astype(jnp.bfloat16)

def token_priors(hidden, head_weight, targets):
    span = math.gcd(TOKENS, 256)

    def one_block(pair):
        rows, wanted = pair
        logits = jnp.dot(rows, head_weight, preferred_element_type=jnp.float32)
        highest = lax.optimization_barrier(jnp.max(logits, axis=-1))
        totals = lax.optimization_barrier(jnp.sum(jnp.exp(logits - highest[:, None]), axis=-1))
        picked = jnp.take_along_axis(logits, wanted[:, None].astype(jnp.int32), axis=1)[:, 0]
        return picked - (highest + jnp.log(totals))
    result = lax.map(one_block, (hidden.reshape(TOKENS // span, span, WIDTH), targets.reshape(TOKENS // span, span)))
    return result.reshape(TOKENS)

def reference(block_query, block_key, block_value, block_doc, token_query, token_key, token_value, token_state, norm_gain, head_weight, targets):
    block_context = global_mixing(block_query, block_key, block_value, block_doc)
    hidden = local_decoder(block_context, token_query, token_key, token_value, token_state, norm_gain)
    return (block_context, token_priors(hidden, head_weight, targets))
```

```python
import functools
import math

import jax
import jax.numpy as jnp
from jax import lax
from jax.experimental import pallas as pl
from jax.experimental.pallas import tpu as pltpu
from jax.sharding import Mesh
from jax.sharding import PartitionSpec as P


HEAD_DIM = 128
BLOCK_LEN = 4
CTX = ("ctx_0", "ctx_1", "ctx_2")
VOCAB = ("vocab_0", "vocab_1")
CTX_VOCAB = ("ctx_0", "ctx_1", "ctx_2", "vocab_0", "vocab_1")

big_negative = -1e30
LANES = 128
K_STEP = 1536


def moved(value, step):
    pairs = []
    for yh in range(2):
        for x in range(4):
            for c in range(2):
                for yl in range(2):
                    for z in range(4):
                        x2, y2, z2, c2 = step(x, yh * 2 + yl, z, c)
                        x2, y2, z2 = x2 % 4, y2 % 4, z2 % 4
                        src = (((yh * 4 + x) * 2 + c) * 2 + yl) * 4 + z
                        dst = ((((y2 // 2) * 4 + x2) * 2 + c2) * 2 + y2 % 2) * 4 + z2
                        pairs.append((src, dst))
    return lax.ppermute(value, CTX_VOCAB, pairs)


def swapped(value):
    return moved(value, lambda x, y, z, c: (x, y, z, 1 - c))


def along_z(value, d):
    return moved(value, lambda x, y, z, c: (x, y, z + d, c))


def second(value, d):
    return moved(value, lambda x, y, z, c: (x + d * c, y + d * (1 - c), z, c))


def third(value, d):
    return moved(value, lambda x, y, z, c: (x + d * (1 - c), y + d * c, z, c))


def ring_pieces(value, send):
    half = value.shape[0] // 2
    lower = send(value, 1)
    upper = send(value, -1)
    first = send(lower[:half], 1)
    last = send(upper[half:], -1)
    return lower, upper, first, last


def score_kernel(rows, *refs):
    wanted_ref = refs[0]
    pieces = refs[1 : 1 + len(rows)]
    w_ref, out_ref, acc_ref, all_ref = refs[1 + len(rows) :]
    step = pl.program_id(0)
    at = 0
    for piece, count in zip(pieces, rows):
        all_ref[at : at + count, :] = piece[...]
        at += count
    part = jnp.dot(all_ref[...], w_ref[...], preferred_element_type=jnp.float32)

    @pl.when(step == 0)
    def _():
        acc_ref[...] = part

    @pl.when(step > 0)
    def _():
        acc_ref[...] += part

    @pl.when(step == pl.num_programs(0) - 1)
    def _():
        span = 128
        for at in range(0, acc_ref.shape[0], span):
            logits = acc_ref[at : at + span, :]
            top = jnp.max(logits, axis=-1, keepdims=True)
            mass = jnp.sum(jnp.exp(logits - top), axis=-1, keepdims=True)
            column = lax.broadcasted_iota(jnp.int32, logits.shape, 1)
            here = column == wanted_ref[at : at + span, :]
            picked = jnp.sum(jnp.where(here, logits, 0.0), axis=-1, keepdims=True)
            lane = lax.broadcasted_iota(jnp.int32, (span, LANES), 1)
            out_ref[at : at + span, :] = jnp.where(
                lane == 0, top, jnp.where(lane == 1, mass, picked)
            )


def scored(wanted, pieces, head_weight):
    rows = tuple(piece.shape[0] for piece in pieces)
    total = sum(rows)
    depth, columns = head_weight.shape
    return pl.pallas_call(
        functools.partial(score_kernel, rows),
        out_shape=jax.ShapeDtypeStruct((total, LANES), jnp.float32),
        grid=(depth // K_STEP,),
        in_specs=[pl.BlockSpec((total, 1), lambda k: (0, 0))]
        + [pl.BlockSpec((r, K_STEP), lambda k: (0, k)) for r in rows]
        + [pl.BlockSpec((K_STEP, columns), lambda k: (k, 0))],
        out_specs=pl.BlockSpec((total, LANES), lambda k: (0, 0)),
        scratch_shapes=[
            pltpu.VMEM((total, columns), jnp.float32),
            pltpu.VMEM((total, K_STEP), jnp.bfloat16),
        ],
        cost_estimate=pl.CostEstimate(
            flops=2 * total * depth * columns,
            transcendentals=total * columns,
            bytes_accessed=2 * depth * (total + columns),
        ),
        name="scored",
    )(wanted, *pieces, head_weight)


def local_decoder(context, token_query, token_key, token_value, token_state, norm_gain):
    scale = 1.0 / math.sqrt(HEAD_DIM)
    groups = context.shape[0]
    width = context.shape[1]
    head_total = width // HEAD_DIM
    shape = (groups, BLOCK_LEN, head_total, HEAD_DIM)
    prefix = context.reshape(groups, 1, head_total, HEAD_DIM)
    queries = token_query.reshape(shape)
    keys = jnp.concatenate([prefix, token_key.reshape(shape)], axis=1)
    values = jnp.concatenate([prefix, token_value.reshape(shape)], axis=1)
    scores = (
        jnp.einsum("bihd,bjhd->bhij", queries, keys, preferred_element_type=jnp.float32) * scale
    )
    allowed = (
        jnp.arange(BLOCK_LEN + 1, dtype=jnp.int32)[None, :]
        <= jnp.arange(BLOCK_LEN, dtype=jnp.int32)[:, None] + 1
    )
    scores = jnp.where(allowed, scores, -jnp.inf)
    highest = jnp.max(scores, axis=-1, keepdims=True)
    weights = jnp.exp(scores - highest)
    totals = jnp.sum(weights, axis=-1)
    mixed = jnp.einsum(
        "bhij,bjhd->bihd", weights.astype(jnp.bfloat16), values, preferred_element_type=jnp.float32
    )
    mixed = mixed / jnp.transpose(totals, (0, 2, 1))[..., None]
    summed = token_state.astype(jnp.float32) + mixed.reshape(groups * BLOCK_LEN, width)
    power = jnp.mean(summed * summed, axis=-1, keepdims=True)
    return (summed * lax.rsqrt(power + 1e-05) * norm_gain).astype(jnp.bfloat16)


def gathered_blocks(block_key, block_value, block_doc):
    rows, width = block_key.shape
    row = jnp.arange(rows, dtype=jnp.int32)
    lane = jnp.arange(LANES, dtype=jnp.int32)[None, :]
    place = lax.axis_index(CTX)
    facts = jnp.where(
        lane == 0, block_doc[:, None], jnp.where(lane == 1, place, row[:, None])
    ).astype(jnp.bfloat16)
    own = jnp.concatenate([block_key, block_value, facts], axis=1)
    across = moved(own, lambda x, y, z, c: (x, y + 2, z, c))
    mine = jnp.concatenate([own, across])
    chip = jnp.concatenate([mine, swapped(mine)])

    def by_core(x, y, z, c):
        return (x + 1 - 2 * c, y, z, c)

    near = moved(chip, by_core)
    far = moved(near[: mine.shape[0]], by_core)
    found = jnp.concatenate([chip, near, swapped(near), far, swapped(far)])
    facts = found[:, 2 * width :].astype(jnp.int32)
    docs = facts[:, 0]
    places = facts[:, 1] * rows + facts[:, 2]
    return found[:, :width], found[:, width : 2 * width], docs, places


def local(
    block_query,
    block_key,
    block_value,
    block_doc,
    token_query,
    token_key,
    token_value,
    token_state,
    norm_gain,
    head_weight,
    targets,
):
    local_rows = block_query.shape[0]
    head_count = block_query.shape[1] // HEAD_DIM
    scale = 1.0 / math.sqrt(HEAD_DIM)
    queries = block_query.reshape(local_rows, head_count, HEAD_DIM)
    query_places = lax.axis_index(CTX) * local_rows + jnp.arange(local_rows, dtype=jnp.int32)
    keys, values, docs, key_places = gathered_blocks(block_key, block_value, block_doc)
    count = keys.shape[0]
    keys = keys.reshape(count, head_count, HEAD_DIM)
    values = values.reshape(count, head_count, HEAD_DIM)
    scores = jnp.einsum("qhd,khd->qhk", queries, keys, preferred_element_type=jnp.float32) * scale
    allowed = (query_places[:, None] >= key_places[None, :]) & (
        block_doc[:, None] == docs[None, :]
    )
    allowed = allowed[:, None, :]
    newest = jnp.max(jnp.where(allowed, scores, big_negative), axis=-1)
    weights = jnp.where(allowed, jnp.exp(scores - newest[..., None]), 0.0)
    totals = jnp.sum(weights, axis=-1)
    mixed = jnp.einsum(
        "qhk,khd->qhd", weights.astype(jnp.bfloat16), values, preferred_element_type=jnp.float32
    )
    block_context = (
        (mixed / totals[..., None]).reshape(local_rows, head_count * HEAD_DIM).astype(jnp.bfloat16)
    )
    grouped = lax.all_to_all(block_context, VOCAB, split_axis=0, concat_axis=1, tiled=True)
    hidden = local_decoder(grouped, token_query, token_key, token_value, token_state, norm_gain)

    own_count = hidden.shape[0]
    yh, x, c, yl, z = (lax.axis_index(name) for name in CTX_VOCAB)
    y = yh * 2 + yl
    offset = jnp.array([0, -1, 1, 2], jnp.int32)
    call_third = jnp.array([[0] * 4, [-1, -1, 1, 1], [-1, -1, 1, 1], [2] * 4], jnp.int32)
    call_second = jnp.array(
        [[0, -1, 1, 2], [0, -1, 1, 2], [1, 2, 0, -1], [0, -1, 1, 2]], jnp.int32
    )
    d3, core, d2, d1 = (
        call_third[:, None, :, None],
        jnp.stack([c, 1 - c])[None, :, None, None],
        call_second[:, None, :, None],
        offset[None, None, None, :],
    )
    x_of = (x + jnp.where(core == 0, d3, d2)) % 4
    y_of = (y + jnp.where(core == 0, d2, d3)) % 4
    z_of = (z + d1) % 4
    ids = ((((y_of // 2) * 4 + x_of) * 2 + core) * 2 + y_of % 2) * 4 + z_of
    devices = ids.size
    ids = ids.reshape(devices)
    spread = (ids[:, None] == jnp.arange(devices, dtype=jnp.int32)[None, :]).astype(jnp.float32)
    wanted = jnp.dot(
        spread, targets.reshape(devices, own_count).astype(jnp.float32), precision="highest"
    ).astype(jnp.int32)
    vocab_cols = head_weight.shape[1]
    wanted = wanted - lax.axis_index(CTX_VOCAB) * vocab_cols
    wanted = wanted.reshape(4, -1, 1)

    line = [hidden, along_z(hidden, 1), along_z(hidden, -1), along_z(hidden, 2)]
    line = jnp.concatenate(line)
    plane = jnp.concatenate([line, *ring_pieces(line, second)])
    half = plane.shape[0] // 2

    lower_0 = third(plane[:half], 1)
    upper_1 = third(plane[half:], -1)
    lower_1 = third(plane[half:], 1)
    upper_0 = third(plane[:half], -1)
    first = third(lower_0, 1)
    last = third(upper_1, -1)
    results = []
    for k, pieces in enumerate(([plane], [lower_0, upper_1], [lower_1, upper_0], [first, last])):
        others = [swapped(piece) for piece in pieces]
        results.append(scored(wanted[k], [*pieces, *others], head_weight))
    stats = jnp.concatenate(results)[:, :3]
    stats = stats.reshape(devices, own_count, 3).transpose(0, 2, 1).reshape(devices, 3 * own_count)
    stats = jnp.dot(spread.T, stats, precision="highest")
    stats = lax.all_to_all(stats, CTX_VOCAB, split_axis=0, concat_axis=0, tiled=True)
    stats = stats.reshape(devices, 3, own_count)
    tops = stats[:, 0]
    top = jnp.max(tops, axis=0)
    mass = jnp.sum(stats[:, 1] * jnp.exp(tops - top), axis=0)
    token_prior = jnp.sum(stats[:, 2], axis=0) - (top + jnp.log(mass))
    return (block_context, token_prior)


def solution(mesh):
    torus = Mesh(
        mesh.devices.reshape(2, 4, 2, 2, 4), ("ctx_0", "ctx_1", "ctx_2", "vocab_0", "vocab_1")
    )
    in_specs = (
        P(CTX, VOCAB),
        P(CTX, VOCAB),
        P(CTX, VOCAB),
        P(CTX),
        P(CTX_VOCAB, None),
        P(CTX_VOCAB, None),
        P(CTX_VOCAB, None),
        P(CTX_VOCAB, None),
        P(),
        P(None, CTX_VOCAB),
        P(),
    )
    out_specs = (P(CTX, VOCAB), P(CTX_VOCAB))
    return jax.shard_map(local, mesh=torus, in_specs=in_specs, out_specs=out_specs, check_vma=False)
```
